512 devices in a mesh: tok: 16 (over z_hi, y), feat: 32 (over x, z_lo, core).
Axes of the slice: x: 4, y: 4, z: 16 (z_hi: 4, z_lo: 4; z = z_hi * 4 + z_lo), core: 2. Of those that a mesh axis runs over, the one named last changes fastest.
Arguments:
- tokens: bfloat16 [1024, 8192], P('tok', 'feat'), may hold values from -6 to 6
- gain: float32 [8192], replicated, may hold values from 0.1 to 1.9
- proj: bfloat16 [8192, 8192], P('tok', 'feat'), may hold values from -0.0625 to 0.0625
- panel_index: int32 [1], replicated, may hold values from 0 to 31
Outputs:
- panel_rows: float32 [256, 8192], P(None, 'feat')
- solved_cross: float32 [256, 8192], P(None, 'feat')
The draws below stay inside these ranges and needn't reach their ends.
All inputs are finite; a program needn't handle non-finite values.
Results may differ from the reference program's by a relative error of at most 0.01.
Values may be sent and summed in bfloat16 or wider, within the bound.
No kernel may reach another device: no remote copies, remote signals or barrier semaphores. Data moves between devices by JAX's collectives and lax.ppermute only.
A program may use at most 64 MiB of HBM per device.

```python
import math
import jax
import jax.numpy as jnp
from jax import lax

D = 8192
PANEL = 256
TOKENS = 1024


def steps_of(own_key, dims, shards, low, largest):
    level, own = 1.0, jax.random.fold_in(own_key, 6)
    for axis_at, blocks in shards:
        draws = jnp.exp(jax.random.uniform(jax.random.fold_in(own, axis_at), (blocks,), jnp.float32, low / len(shards), largest / len(shards)))
        level = level * jnp.repeat(draws, dims[axis_at] // blocks).reshape([-1 if axis == axis_at else 1 for axis in range(len(dims))])
    return level


def normal_values(rng, shape, scale, reach, split=(), kind=jnp.bfloat16):
    drawn = scale * jax.random.normal(rng, shape, jnp.float32)
    if split:
        drawn = drawn * steps_of(rng, shape, split, -0.22, 0.18)
    return jnp.clip(drawn, -reach, reach).astype(kind)


def setup_inputs(seed: int = 0) -> dict:
    streams_of = jax.random.split(jax.random.key(seed), 5)
    return {
        "tokens": normal_values(streams_of[0], (TOKENS, D), 1.0, 6.0, ((0, 16), (1, 32))),
        "gain": jnp.clip(1.0 + 0.18 * jax.random.normal(streams_of[1], (D,), jnp.float32), 0.1, 1.9),
        "proj": normal_values(streams_of[2], (D, D), D ** -0.5, 0.0625, ((0, 16), (1, 32))),
        "panel_index": jax.random.randint(streams_of[3], (1,), 0, D // PANEL).astype(jnp.int32),
    }


def reference(tokens, gain, proj, panel_index):
    values = tokens.astype(jnp.float32)
    inv_rms = lax.rsqrt(lax.optimization_barrier(jnp.mean(values * values, axis=1, keepdims=True)) + 1e-05)
    normed = (values * inv_rms * gain[None, :]).astype(jnp.bfloat16)
    outputs = (values + jnp.dot(normed.astype(jnp.float32), proj.astype(jnp.float32), preferred_element_type=jnp.float32)).astype(jnp.bfloat16)
    change = (outputs.astype(jnp.float32) - values).astype(jnp.bfloat16)
    band_start = panel_index[0].astype(jnp.int32) * PANEL
    band_cols = lax.dynamic_slice_in_dim(tokens, band_start, PANEL, 1)
    token_count = tokens.shape[0]
    gram_rows = jnp.dot(band_cols.T.astype(jnp.float32), tokens.astype(jnp.float32), preferred_element_type=jnp.float32) / token_count
    row_ids = lax.broadcasted_iota(jnp.int32, (PANEL, D), 0)
    col_ids = lax.broadcasted_iota(jnp.int32, (PANEL, D), 1)
    ridge_mask = jnp.where(col_ids == row_ids + band_start, 0.1, 0.0).astype(jnp.float32)
    gram_rows = gram_rows + ridge_mask
    cross_rows = jnp.dot(band_cols.T.astype(jnp.float32), change.astype(jnp.float32), preferred_element_type=jnp.float32) * (math.sqrt(D) / token_count)
    diag_block = lax.dynamic_slice_in_dim(gram_rows, band_start, PANEL, 1)
    factor = jnp.linalg.cholesky(diag_block)
    panel_rows = lax.linalg.triangular_solve(factor, gram_rows, left_side=True, lower=True)
    solved_cross = lax.linalg.triangular_solve(factor, cross_rows, left_side=True, lower=True)
    return (panel_rows, solved_cross)
```

```python
import functools
import math

import jax
import jax.numpy as jnp
import numpy as np
from jax import lax
from jax.experimental import pallas as pl
from jax.experimental.pallas import tpu as pltpu
from jax.sharding import Mesh
from jax.sharding import PartitionSpec as P

D = 8192
PANEL = 256
TOKENS = 1024
AXES = ("zh", "y", "x", "zl", "c")
TOK = ("zh", "y")
FEAT = ("x", "zl", "c")
NB = 64
F32 = jnp.float32
BF16 = jnp.bfloat16
HIGHEST = lax.Precision.HIGHEST


def swap(value, axis, bits, size=4):
    return lax.ppermute(value, axis, [(i, i ^ bits) for i in range(size)])


def call(kernel, outs, *args, n_scalars=0, scratch=()):
    vmem = pl.BlockSpec(memory_space=pltpu.VMEM)
    smem = pl.BlockSpec(memory_space=pltpu.SMEM)
    many = isinstance(outs, tuple)
    return pl.pallas_call(
        kernel,
        out_shape=outs,
        in_specs=[smem] * n_scalars + [vmem] * (len(args) - n_scalars),
        out_specs=tuple(vmem for _ in outs) if many else vmem,
        scratch_shapes=list(scratch),
    )(*args)


def dot_tn(a, b):
    return lax.dot_general(a, b, (((0,), (0,)), ((), ())), preferred_element_type=F32)


def project_kernel(pos, mine, other, gain, p0, p1, p2, p3, keep, s1, s2, s3, acc, sq):
    zh, y, x, zl, c = pos[0], pos[1], pos[2], pos[3], pos[4]
    total = jnp.zeros((256, 256), F32)
    squares = jnp.zeros((256, 256), F32)
    for y_rel, proj in enumerate((p0, p1, p2, p3)):
        zl_there = y ^ y_rel
        z_rel = zl ^ zl_there
        for c_rel, src in enumerate((mine, other)):
            c_there = c ^ c_rel
            rows = [
                src[pl.ds(pl.multiple_of(64 + (x_rel * 4 + z_rel) * 64, 64), 64), :]
                for x_rel in range(4)
            ]
            raw = jnp.concatenate(rows, axis=0).astype(F32)
            squares = squares + raw * raw
            scale = gain[pl.ds(8 * zh + 2 * zl_there + c_there, 1), :]
            scaled = (raw * scale).astype(BF16)
            weights = proj[pl.ds(pl.multiple_of(c_there * 256, 256), 256), :]
            total = total + jnp.dot(scaled, weights, preferred_element_type=F32)
    acc[...] = total
    sq[...] = jnp.broadcast_to(jnp.sum(squares, axis=1, keepdims=True), (256, 256))
    row = lax.broadcasted_iota(jnp.int32, (64, 256), 0)
    lane = lax.broadcasted_iota(jnp.int32, (64, 256), 1)
    for step, out in enumerate((keep, s1, s2, s3)):
        at = pl.multiple_of((x ^ zh ^ step) * 64, 64)
        part = acc[pl.ds(at, 64), :]
        own = sq[pl.ds(at, 64), :]
        high = own.astype(BF16).astype(F32)
        spread = jnp.where(lane == row, high, jnp.where(lane == row + 64, own - high, 0.0))
        line = jnp.sum(spread, axis=0, keepdims=True)
        out[0:64, :] = part.astype(out.dtype)
        out[64:80, :] = jnp.broadcast_to(line, (16, 256)).astype(out.dtype)


def change_kernel(tokens, keep, r1, r2, r3, change):
    total = keep[...] + r1[...].astype(F32) + r2[...].astype(F32) + r3[...].astype(F32)
    row = lax.broadcasted_iota(jnp.int32, (64, 256), 0)
    lane = lax.broadcasted_iota(jnp.int32, (64, 256), 1)
    line = jnp.broadcast_to(total[64:65, :], (64, 256))
    picked = jnp.where((lane == row) | (lane == row + 64), line, 0.0)
    square_sum = jnp.sum(picked, axis=1, keepdims=True)
    inv_rms = lax.rsqrt(square_sum / D + 1e-05)
    own = tokens[...].astype(F32)
    outputs = (own + total[0:64, :] * inv_rms).astype(BF16)
    change[...] = (outputs.astype(F32) - own).astype(BF16)


def invert_block(block):
    row = lax.broadcasted_iota(jnp.int32, (NB, 2 * NB), 0)
    lane = lax.broadcasted_iota(jnp.int32, (NB, 2 * NB), 1)
    eye = jnp.where(lane[:, :NB] == row[:, :NB], 1.0, 0.0).astype(F32)
    work = jnp.concatenate([block, eye], axis=1)
    for j in range(NB):
        column = jnp.broadcast_to(work[:, j : j + 1], (NB, 2 * NB))
        scale = lax.rsqrt(column[j : j + 1, :])
        pivot = work[j : j + 1, :] * scale
        lower = jnp.where(row > j, column * scale, 0.0)
        work = jnp.where(row == j, pivot, work - lower * pivot)
    return work[:, NB:]


def dot_hi(a, b, dims=((1,), (0,))):
    return lax.dot_general(a, b, (dims, ((), ())), precision=HIGHEST, preferred_element_type=F32)


def factor_kernel(b0, b1, b2, b3, inverse, schur):
    total = dot_tn(b0[:, 0:256], b0[:, 0:256])
    for b in (b1, b2, b3):
        total = total + dot_tn(b[:, 0:256], b[:, 0:256])
    row = lax.broadcasted_iota(jnp.int32, (PANEL, PANEL), 0)
    lane = lax.broadcasted_iota(jnp.int32, (PANEL, PANEL), 1)
    schur[...] = total / TOKENS + jnp.where(row == lane, 0.1, 0.0)
    inverse[...] = jnp.where(row == lane, 1.0, 0.0)
    for k in range(PANEL // NB):
        lo, hi = k * NB, (k + 1) * NB
        block_inverse = invert_block(schur[lo:hi, lo:hi])
        top = dot_hi(block_inverse, inverse[lo:hi, :])
        inverse[lo:hi, :] = top
        if hi < PANEL:
            below = dot_hi(schur[hi:, lo:hi], block_inverse, ((1,), (1,)))
            schur[hi:, hi:] = schur[hi:, hi:] - dot_hi(below, below, ((1,), (1,)))
            inverse[hi:, :] = inverse[hi:, :] - dot_hi(below, top)


def gram_kernel(is_band, b0, b1, b2, b3, inverse, out):
    total = dot_tn(b0[:, 0:256], b0[:, 256:512])
    for b in (b1, b2, b3):
        total = total + dot_tn(b[:, 0:256], b[:, 256:512])
    row = lax.broadcasted_iota(jnp.int32, (PANEL, PANEL), 0)
    lane = lax.broadcasted_iota(jnp.int32, (PANEL, PANEL), 1)
    ridge = jnp.where((row == lane) & (is_band[0] == 1), 0.1, 0.0)
    out[...] = dot_hi(inverse[...], total / TOKENS + ridge)


def cross_kernel(b0, b1, b2, b3, c0, c1, c2, c3, inverse, out):
    total = dot_tn(b0[:, 0:256], c0[...])
    for b, change in ((b1, c1), (b2, c2), (b3, c3)):
        total = total + dot_tn(b[:, 0:256], change[...])
    out[...] = dot_hi(inverse[...], total * (math.sqrt(D) / TOKENS))


def gather_tok(value):
    first = [value] + [swap(value, "zh", k) for k in (2, 1, 3)]
    quarter = jnp.concatenate(first, axis=0)
    return [quarter] + [swap(quarter, "y", k) for k in (2, 1, 3)]


def body(tokens, gain, proj, panel_index):
    place = [lax.axis_index(a).astype(jnp.int32) for a in AXES]
    zh, y, x, zl, c = place
    is_band = panel_index[0].astype(jnp.int32) == 8 * x + 2 * zl + c
    band = jnp.where(is_band, tokens, jnp.zeros_like(tokens))

    turned = lax.ppermute(
        tokens,
        AXES,
        [
            ((((a * 4 + b) * 4 + d) * 8 + e), (((d * 4 + b) * 4 + a) * 8 + e))
            for a in range(4)
            for b in range(4)
            for d in range(4)
            for e in range(8)
        ],
    )
    weights = [proj] + [swap(proj, "y", k) for k in (1, 2, 3)]

    load = jnp.concatenate([band, turned], axis=0)
    others = [swap(load, "zl", k) for k in (1, 2, 3)]
    band = band + others[0][:64] + others[1][:64] + others[2][:64]
    load = jnp.concatenate([band, turned] + [o[64:] for o in others], axis=0)
    others = [swap(load, "x", k) for k in (1, 2, 3)]
    band = band + others[0][:64] + others[1][:64] + others[2][:64]
    load = jnp.concatenate([band, load[64:]] + [o[64:] for o in others], axis=0)
    other = swap(load, "c", 1, 2)
    band = band + other[:64]

    part = jax.ShapeDtypeStruct((80, 256), BF16)
    keep, s1, s2, s3 = call(
        project_kernel,
        (jax.ShapeDtypeStruct((80, 256), F32), part, part, part),
        jnp.stack(place),
        load,
        other,
        gain.reshape(32, 256),
        *weights,
        n_scalars=1,
        scratch=(pltpu.VMEM((256, 256), F32), pltpu.VMEM((256, 256), F32)),
    )
    r2, r1, r3 = swap(s2, "zh", 2), swap(s1, "zh", 1), swap(s3, "zh", 3)
    change = call(change_kernel, jax.ShapeDtypeStruct((64, 256), BF16), tokens, keep, r1, r2, r3)

    pairs = gather_tok(jnp.concatenate([band, tokens], axis=1))
    changes = gather_tok(change)

    square = jax.ShapeDtypeStruct((PANEL, PANEL), F32)
    inverse = call(factor_kernel, square, *pairs, scratch=(pltpu.VMEM((PANEL, PANEL), F32),))
    panel_rows = call(
        gram_kernel, square, is_band.astype(jnp.int32).reshape(1), *pairs, inverse, n_scalars=1
    )
    solved_cross = call(cross_kernel, square, *pairs, *changes, inverse)
    return (panel_rows, solved_cross)


def solution(mesh):
    split = Mesh(np.asarray(mesh.devices).reshape(4, 4, 4, 4, 2), AXES)
    return jax.shard_map(
        body,
        mesh=split,
        in_specs=(P(TOK, FEAT), P(), P(TOK, FEAT), P()),
        out_specs=(P(None, FEAT), P(None, FEAT)),
        check_vma=False,
    )
```

```python
import math

import jax
import jax.numpy as jnp
import numpy as np
from jax import lax
from jax.experimental import pallas as pl
from jax.experimental.pallas import tpu as pltpu
from jax.sharding import Mesh
from jax.sharding import PartitionSpec as P

D = 8192
PANEL = 256
TOKENS = 1024
AXES = ("zh", "y", "x", "zl", "c")
TOK = ("zh", "y")
FEAT = ("x", "zl", "c")
NB = 64
STEP = 8
F32 = jnp.float32
BF16 = jnp.bfloat16
HIGHEST = lax.Precision.HIGHEST


def swap(value, axis, bits, size=4):
    return lax.ppermute(value, axis, [(i, i ^ bits) for i in range(size)])


def double(value, axis, bits):
    return jnp.concatenate([value, swap(value, axis, bits)], axis=0)


def merge(mine, other):
    return jnp.concatenate([mine[:64] + other[:64], mine[64:], other[64:]], axis=0)


def call(kernel, outs, *args, n_scalars=0, scratch=(), final=False):
    vmem = pl.BlockSpec(memory_space=pltpu.VMEM)
    smem = pl.BlockSpec(memory_space=pltpu.SMEM)
    many = isinstance(outs, tuple)
    args = args[:n_scalars] + tuple(
        pltpu.with_memory_space_constraint(a, pltpu.VMEM) for a in args[n_scalars:]
    )
    if not final:
        kept = [pltpu.VMEM(o.shape, o.dtype) for o in (outs if many else (outs,))]
        outs = tuple(kept) if many else kept[0]
    return pl.pallas_call(
        kernel,
        out_shape=outs,
        in_specs=[smem] * n_scalars + [vmem] * (len(args) - n_scalars),
        out_specs=tuple(vmem for _ in outs) if many else vmem,
        scratch_shapes=list(scratch),
    )(*args)


def dot_tn(a, b):
    return lax.dot_general(a, b, (((0,), (0,)), ((), ())), preferred_element_type=F32)


def project_kernel(mine, other, gain, p0, p1, far, keep, s1, s2, s3, acc, sq):
    zh, y, x, zl, c = [lax.axis_index(a) for a in AXES]
    total = jnp.zeros((256, 256), F32)
    squares = jnp.zeros((256, 256), F32)
    for y_rel, (proj, at) in enumerate(((p0, 0), (p1, 0), (far, 512), (far, 0))):
        zl_there = y ^ y_rel
        z_rel = zl ^ zl_there
        for c_rel, src in enumerate((mine, other)):
            c_there = c ^ c_rel
            rows = [
                src[pl.ds(pl.multiple_of(64 + (at_x * 4 + z_rel) * 64, 64), 64), :]
                for at_x in (0, 1, 3, 2)
            ]
            raw = jnp.concatenate(rows, axis=0).astype(F32)
            squares = squares + raw * raw
            scale = gain[pl.ds(8 * zh + 2 * zl_there + c_there, 1), :]
            scaled = (raw * scale).astype(BF16)
            weights = proj[pl.ds(pl.multiple_of(at + c_there * 256, 256), 256), :]
            total = total + jnp.dot(scaled, weights, preferred_element_type=F32)
    acc[...] = total
    sq[...] = jnp.broadcast_to(jnp.sum(squares, axis=1, keepdims=True), (256, 256))
    row = lax.broadcasted_iota(jnp.int32, (64, 256), 0)
    lane = lax.broadcasted_iota(jnp.int32, (64, 256), 1)
    for step, out in enumerate((keep, s1, s2, s3)):
        at = pl.multiple_of((x ^ zh ^ step) * 64, 64)
        part = acc[pl.ds(at, 64), :]
        norm = sq[pl.ds(at, 64), :]
        high = norm.astype(BF16).astype(F32)
        spread = jnp.where(lane == row, high, jnp.where(lane == row + 64, norm - high, 0.0))
        line = jnp.sum(spread, axis=0, keepdims=True)
        out[0:64, :] = part.astype(out.dtype)
        out[64:80, :] = jnp.broadcast_to(line, (16, 256)).astype(out.dtype)
        if step:
            out[80:144, :] = mine[0:64, :] + other[0:64, :]


def change_kernel(tokens, keep, r1, r2, r3, change):
    total = keep[...]
    for part in (r1, r2, r3):
        total = total + part[0:80, :].astype(F32)
    row = lax.broadcasted_iota(jnp.int32, (64, 256), 0)
    lane = lax.broadcasted_iota(jnp.int32, (64, 256), 1)
    line = jnp.broadcast_to(total[64:65, :], (64, 256))
    picked = jnp.where((lane == row) | (lane == row + 64), line, 0.0)
    square_sum = jnp.sum(picked, axis=1, keepdims=True)
    inv_rms = lax.rsqrt(square_sum / D + 1e-05)
    own = tokens[...].astype(F32)
    outputs = (own + total[0:64, :] * inv_rms).astype(BF16)
    change[...] = (outputs.astype(F32) - own).astype(BF16)


def invert_block(block):
    row = lax.broadcasted_iota(jnp.int32, (NB, 2 * NB), 0)
    lane = lax.broadcasted_iota(jnp.int32, (NB, 2 * NB), 1)
    eye = jnp.where(lane[:, :NB] == row[:, :NB], 1.0, 0.0).astype(F32)
    work = jnp.concatenate([block, eye], axis=1)
    for j in range(0, NB, STEP):
        columns = [jnp.broadcast_to(work[:, k : k + 1], work.shape) for k in range(j, j + STEP)]
        pivots = [work[k : k + 1, :] for k in range(j, j + STEP)]
        for i in range(STEP):
            scale = lax.rsqrt(columns[i][j + i : j + i + 1, :])
            pivots[i] = pivots[i] * scale
            columns[i] = columns[i] * scale
            for k in range(i + 1, STEP):
                factor = columns[i][j + k : j + k + 1, :]
                pivots[k] = pivots[k] - factor * pivots[i]
                columns[k] = columns[k] - factor * columns[i]
        update = columns[0] * pivots[0]
        for i in range(1, STEP):
            update = update + columns[i] * pivots[i]
        after = jnp.where(row >= j + STEP, work - update, work)
        for i in range(STEP):
            after = jnp.where(row == j + i, pivots[i], after)
        work = after
    return work[:, NB:]


def dot_hi(a, b, dims=((1,), (0,))):
    return lax.dot_general(a, b, (dims, ((), ())), precision=HIGHEST, preferred_element_type=F32)


def factor_kernel(b0, b1, inverse, schur):
    total = dot_tn(b0[...], b0[...]) + dot_tn(b1[...], b1[...])
    row = lax.broadcasted_iota(jnp.int32, (PANEL, PANEL), 0)
    lane = lax.broadcasted_iota(jnp.int32, (PANEL, PANEL), 1)
    schur[...] = total / TOKENS + jnp.where(row == lane, 0.1, 0.0)
    inverse[...] = jnp.where(row == lane, 1.0, 0.0)
    for k in range(PANEL // NB):
        lo, hi = k * NB, (k + 1) * NB
        block_inverse = invert_block(schur[lo:hi, lo:hi])
        top = dot_hi(block_inverse, inverse[lo:hi, :])
        inverse[lo:hi, :] = top
        if hi < PANEL:
            below = dot_hi(schur[hi:, lo:hi], block_inverse, ((1,), (1,)))
            schur[hi:, hi:] = schur[hi:, hi:] - dot_hi(below, below, ((1,), (1,)))
            inverse[hi:, :] = inverse[hi:, :] - dot_hi(below, top)


def gram_kernel(is_band, b0, b1, t0, t1, inverse, out):
    total = dot_tn(b0[...], t0[...]) + dot_tn(b1[...], t1[...])
    row = lax.broadcasted_iota(jnp.int32, (PANEL, PANEL), 0)
    lane = lax.broadcasted_iota(jnp.int32, (PANEL, PANEL), 1)
    ridge = jnp.where((row == lane) & (is_band[0] == 1), 0.1, 0.0)
    out[...] = dot_hi(inverse[...], total / TOKENS + ridge)


def cross_kernel(b0, b1, c0, c1, c2, c3, inverse, out):
    total = dot_tn(b0[0:256, :], c0[...]) + dot_tn(b0[256:512, :], c1[...])
    total = total + dot_tn(b1[0:256, :], c2[...]) + dot_tn(b1[256:512, :], c3[...])
    out[...] = dot_hi(inverse[...], total * (math.sqrt(D) / TOKENS))


def steps(tokens, gain, proj, panel_index):
    _, _, x, zl, c = [lax.axis_index(a).astype(jnp.int32) for a in AXES]
    is_band = panel_index[0].astype(jnp.int32) == 8 * x + 2 * zl + c
    band = jnp.where(is_band, tokens, jnp.zeros_like(tokens))
    gains = gain.reshape(32, 256)

    turned = lax.ppermute(
        tokens,
        AXES,
        [
            ((((a * 4 + b) * 4 + d) * 8 + e), (((d * 4 + b) * 4 + a) * 8 + e))
            for a in range(4)
            for b in range(4)
            for d in range(4)
            for e in range(8)
        ],
    )
    weights = [proj, swap(proj, "y", 1)]

    load = jnp.concatenate([band, turned], axis=0)
    load, gains = lax.optimization_barrier((load, gains))
    load = merge(load, swap(load, "zl", 1))
    load, weights = lax.optimization_barrier((load, weights))
    weights.append(swap(jnp.concatenate(weights, axis=0), "y", 3))
    load = merge(load, swap(load, "zl", 2))
    there = swap(load, "x", 1)
    blocks = double(tokens, "zh", 1)
    load, blocks = lax.optimization_barrier((merge(load, there), blocks))
    there = swap(load, "x", 3)
    blocks = double(blocks, "zh", 3)
    load = merge(load, there)
    band = load[:64]
    other = swap(load, "c", 1, 2)
    band = band + other[:64]

    part = jax.ShapeDtypeStruct((144, 256), BF16)
    keep, s1, s2, s3 = call(
        project_kernel,
        (jax.ShapeDtypeStruct((80, 256), F32), part, part, part),
        load,
        other,
        gains,
        *weights,
        scratch=(pltpu.VMEM((256, 256), F32), pltpu.VMEM((256, 256), F32)),
    )
    r2, r1, r3 = swap(s2, "zh", 2), swap(s1, "zh", 1), swap(s3, "zh", 3)
    blocks = double(blocks, "y", 1)
    blocks = [blocks, swap(blocks, "y", 3)]
    bands = jnp.concatenate([band] + [r[80:144] for r in (r1, r3, r2)], axis=0)
    bands = double(bands, "y", 1)
    bands = [bands, swap(bands, "y", 3)]

    change = call(change_kernel, jax.ShapeDtypeStruct((64, 256), BF16), tokens, keep, r1, r2, r3)
    change = double(change, "zh", 1)
    change = double(change, "zh", 3)
    changes = [change] + [swap(change, "y", k) for k in (1, 3, 2)]

    square = jax.ShapeDtypeStruct((PANEL, PANEL), F32)
    inverse = call(factor_kernel, square, *bands, scratch=(pltpu.VMEM((PANEL, PANEL), F32),))
    flag = is_band.astype(jnp.int32).reshape(1)
    panel_rows = call(gram_kernel, square, flag, *bands, *blocks, inverse, n_scalars=1, final=True)
    solved_cross = call(cross_kernel, square, *bands, *changes, inverse, final=True)
    return (panel_rows, solved_cross)


def solution(mesh):
    split = Mesh(np.asarray(mesh.devices).reshape(4, 4, 4, 4, 2), AXES)
    return jax.shard_map(
        steps,
        mesh=split,
        in_specs=(P(TOK, FEAT), P(), P(TOK, FEAT), P()),
        out_specs=(P(None, FEAT), P(None, FEAT)),
        check_vma=False,
    )
```

```python
import math

import jax
import jax.numpy as jnp
import numpy as np
from jax import lax
from jax.experimental import pallas as pl
from jax.experimental.pallas import tpu as pltpu
from jax.sharding import Mesh
from jax.sharding import PartitionSpec as P

D = 8192
PANEL = 256
TOKENS = 1024
AXES = ("zh", "y", "x", "zl", "c")
TOK = ("zh", "y")
FEAT = ("x", "zl", "c")
NB = 64
STEP = 16
F32 = jnp.float32
BF16 = jnp.bfloat16
HIGHEST = lax.Precision.HIGHEST


def swap(value, axis, bits, size=4):
    return lax.ppermute(value, axis, [(i, i ^ bits) for i in range(size)])


def double(value, axis, bits):
    return jnp.concatenate([value, swap(value, axis, bits)], axis=0)


def spread(load, axis):
    parts = jnp.broadcast_to(load[None], (4, *load.shape))
    parts = lax.all_to_all(parts, axis, 0, 0, tiled=True)
    band = parts[0, :64] + parts[1, :64] + parts[2, :64] + parts[3, :64]
    return jnp.concatenate([band] + [parts[i, 64:] for i in range(4)], axis=0), band


def call(kernel, outs, *args, n_scalars=0, scratch=(), final=False):
    vmem = pl.BlockSpec(memory_space=pltpu.VMEM)
    smem = pl.BlockSpec(memory_space=pltpu.SMEM)
    many = isinstance(outs, tuple)
    args = args[:n_scalars] + tuple(
        pltpu.with_memory_space_constraint(a, pltpu.VMEM) for a in args[n_scalars:]
    )
    if not final:
        kept = [pltpu.VMEM(o.shape, o.dtype) for o in (outs if many else (outs,))]
        outs = tuple(kept) if many else kept[0]
    return pl.pallas_call(
        kernel,
        out_shape=outs,
        in_specs=[smem] * n_scalars + [vmem] * (len(args) - n_scalars),
        out_specs=tuple(vmem for _ in outs) if many else vmem,
        scratch_shapes=list(scratch),
    )(*args)


def dot_tn(a, b):
    return lax.dot_general(a, b, (((0,), (0,)), ((), ())), preferred_element_type=F32)


def project_kernel(mine, other, gain, p0, p1, p2, p3, keep, s1, s2, s3, acc, sq):
    zh, y, c = [lax.axis_index(a) for a in ("zh", "y", "c")]
    total = jnp.zeros((256, 256), F32)
    squares = jnp.zeros((256, 256), F32)
    for y_rel, proj in enumerate((p0, p1, p2, p3)):
        zl_there = y ^ y_rel
        for c_rel, src in enumerate((mine, other)):
            c_there = c ^ c_rel
            rows = [
                src[pl.ds(pl.multiple_of(64 + (at_x * 4 + zl_there) * 64, 64), 64), :]
                for at_x in range(4)
            ]
            raw = jnp.concatenate(rows, axis=0).astype(F32)
            squares = squares + raw * raw
            scale = gain[pl.ds(8 * zh + 2 * zl_there + c_there, 1), :]
            scaled = (raw * scale).astype(BF16)
            weights = proj[pl.ds(pl.multiple_of(c_there * 256, 256), 256), :]
            total = total + jnp.dot(scaled, weights, preferred_element_type=F32)
    acc[...] = total
    sq[...] = jnp.broadcast_to(jnp.sum(squares, axis=1, keepdims=True), (256, 256))
    row = lax.broadcasted_iota(jnp.int32, (64, 256), 0)
    lane = lax.broadcasted_iota(jnp.int32, (64, 256), 1)
    for step, out in enumerate((keep, s1, s2, s3)):
        at = pl.multiple_of((zh ^ step) * 64, 64)
        part = acc[pl.ds(at, 64), :]
        norm = sq[pl.ds(at, 64), :]
        high = norm.astype(BF16).astype(F32)
        spread = jnp.where(lane == row, high, jnp.where(lane == row + 64, norm - high, 0.0))
        line = jnp.sum(spread, axis=0, keepdims=True)
        out[0:64, :] = part.astype(out.dtype)
        out[64:80, :] = jnp.broadcast_to(line, (16, 256)).astype(out.dtype)
        if step:
            out[80:144, :] = mine[0:64, :] + other[0:64, :]


def change_kernel(tokens, keep, r1, r2, r3, change):
    total = keep[...]
    for part in (r1, r2, r3):
        total = total + part[0:80, :].astype(F32)
    row = lax.broadcasted_iota(jnp.int32, (64, 256), 0)
    lane = lax.broadcasted_iota(jnp.int32, (64, 256), 1)
    line = jnp.broadcast_to(total[64:65, :], (64, 256))
    picked = jnp.where((lane == row) | (lane == row + 64), line, 0.0)
    square_sum = jnp.sum(picked, axis=1, keepdims=True)
    inv_rms = lax.rsqrt(square_sum / D + 1e-05)
    own = tokens[...].astype(F32)
    outputs = (own + total[0:64, :] * inv_rms).astype(BF16)
    change[...] = (outputs.astype(F32) - own).astype(BF16)


def invert_block(block):
    row = lax.broadcasted_iota(jnp.int32, (NB, 2 * NB), 0)
    lane = lax.broadcasted_iota(jnp.int32, (NB, 2 * NB), 1)
    eye = jnp.where(lane[:, :NB] == row[:, :NB], 1.0, 0.0).astype(F32)
    work = jnp.concatenate([block, eye], axis=1)
    for j in range(0, NB, STEP):
        columns = [jnp.broadcast_to(work[:, k : k + 1], work.shape) for k in range(j, j + STEP)]
        pivots = [work[k : k + 1, :] for k in range(j, j + STEP)]
        for i in range(STEP):
            scale = lax.rsqrt(columns[i][j + i : j + i + 1, :])
            pivots[i] = pivots[i] * scale
            columns[i] = columns[i] * scale
            for k in range(i + 1, STEP):
                factor = columns[i][j + k : j + k + 1, :]
                pivots[k] = pivots[k] - factor * pivots[i]
                columns[k] = columns[k] - factor * columns[i]
        update = columns[0] * pivots[0]
        for i in range(1, STEP):
            update = update + columns[i] * pivots[i]
        after = jnp.where(row >= j + STEP, work - update, work)
        for i in range(STEP):
            after = jnp.where(row == j + i, pivots[i], after)
        work = after
    return work[:, NB:]


def dot_hi(a, b, dims=((1,), (0,))):
    return lax.dot_general(a, b, (dims, ((), ())), precision=HIGHEST, preferred_element_type=F32)


def factor_kernel(b0, b1, inverse, schur):
    total = dot_tn(b0[...], b0[...]) + dot_tn(b1[...], b1[...])
    row = lax.broadcasted_iota(jnp.int32, (PANEL, PANEL), 0)
    lane = lax.broadcasted_iota(jnp.int32, (PANEL, PANEL), 1)
    schur[...] = total / TOKENS + jnp.where(row == lane, 0.1, 0.0)
    inverse[...] = jnp.where(row == lane, 1.0, 0.0)
    for k in range(PANEL // NB):
        lo, hi = k * NB, (k + 1) * NB
        block_inverse = invert_block(schur[lo:hi, lo:hi])
        top = dot_hi(block_inverse, inverse[lo:hi, :])
        inverse[lo:hi, :] = top
        if hi < PANEL:
            below = dot_hi(schur[hi:, lo:hi], block_inverse, ((1,), (1,)))
            schur[hi:, hi:] = schur[hi:, hi:] - dot_hi(below, below, ((1,), (1,)))
            inverse[hi:, :] = inverse[hi:, :] - dot_hi(below, top)


def gram_kernel(is_band, b0, b1, t0, t1, inverse, out):
    total = dot_tn(b0[...], t0[...]) + dot_tn(b1[...], t1[...])
    row = lax.broadcasted_iota(jnp.int32, (PANEL, PANEL), 0)
    lane = lax.broadcasted_iota(jnp.int32, (PANEL, PANEL), 1)
    ridge = jnp.where((row == lane) & (is_band[0] == 1), 0.1, 0.0)
    out[...] = dot_hi(inverse[...], total / TOKENS + ridge)


def cross_kernel(b0, b1, c0, c1, c2, c3, inverse, out):
    total = dot_tn(b0[0:256, :], c0[...]) + dot_tn(b0[256:512, :], c1[...])
    total = total + dot_tn(b1[0:256, :], c2[...]) + dot_tn(b1[256:512, :], c3[...])
    out[...] = dot_hi(inverse[...], total * (math.sqrt(D) / TOKENS))


def steps(tokens, gain, proj, panel_index):
    _, _, x, zl, c = [lax.axis_index(a).astype(jnp.int32) for a in AXES]
    is_band = panel_index[0].astype(jnp.int32) == 8 * x + 2 * zl + c
    band = jnp.where(is_band, tokens, jnp.zeros_like(tokens))
    gains = gain.reshape(32, 256)

    turned = lax.ppermute(
        tokens,
        AXES,
        [
            ((((a * 4 + b) * 4 + d) * 8 + e), (((d * 4 + b) * 4 + a) * 8 + e))
            for a in range(4)
            for b in range(4)
            for d in range(4)
            for e in range(8)
        ],
    )
    weights = [proj] + [swap(proj, "y", k) for k in (1, 2, 3)]

    load = jnp.concatenate([band, turned], axis=0)
    load, gains = lax.optimization_barrier((load, gains))
    load, band = spread(load, "zl")
    load, early = lax.optimization_barrier((load, tokens))
    blocks = double(early, "zh", 1)
    load, band = spread(load, "x")
    blocks = double(blocks, "zh", 3)
    other = swap(load, "c", 1, 2)
    band = band + other[:64]

    part = jax.ShapeDtypeStruct((144, 256), BF16)
    keep, s1, s2, s3 = call(
        project_kernel,
        (jax.ShapeDtypeStruct((80, 256), F32), part, part, part),
        load,
        other,
        gains,
        *weights,
        scratch=(pltpu.VMEM((256, 256), F32), pltpu.VMEM((256, 256), F32)),
    )
    r2, r1, r3 = swap(s2, "zh", 2), swap(s1, "zh", 1), swap(s3, "zh", 3)
    blocks = double(blocks, "y", 1)
    blocks = [blocks, swap(blocks, "y", 3)]
    bands = jnp.concatenate([band] + [r[80:144] for r in (r1, r3, r2)], axis=0)
    bands = double(bands, "y", 1)
    bands = [bands, swap(bands, "y", 3)]

    change = call(change_kernel, jax.ShapeDtypeStruct((64, 256), BF16), tokens, keep, r1, r2, r3)
    change = double(change, "zh", 1)
    change = double(change, "zh", 3)
    changes = [change] + [swap(change, "y", k) for k in (1, 3, 2)]

    square = jax.ShapeDtypeStruct((PANEL, PANEL), F32)
    inverse = call(factor_kernel, square, *bands, scratch=(pltpu.VMEM((PANEL, PANEL), F32),))
    flag = is_band.astype(jnp.int32).reshape(1)
    panel_rows = call(gram_kernel, square, flag, *bands, *blocks, inverse, n_scalars=1, final=True)
    solved_cross = call(cross_kernel, square, *bands, *changes, inverse, final=True)
    return (panel_rows, solved_cross)


def solution(mesh):
    split = Mesh(np.asarray(mesh.devices).reshape(4, 4, 4, 4, 2), AXES)
    return jax.shard_map(
        steps,
        mesh=split,
        in_specs=(P(TOK, FEAT), P(), P(TOK, FEAT), P()),
        out_specs=(P(None, FEAT), P(None, FEAT)),
        check_vma=False,
    )
```

```python
import math

import jax
import jax.numpy as jnp
import numpy as np
from jax import lax
from jax.experimental import pallas as pl
from jax.experimental.pallas import tpu as pltpu
from jax.sharding import Mesh
from jax.sharding import PartitionSpec as P

D = 8192
PANEL = 256
TOKENS = 1024
AXES = ("zh", "y", "x", "zl", "c")
TOK = ("zh", "y")
FEAT = ("x", "zl", "c")
NB = 64
STEP = 16
F32 = jnp.float32
BF16 = jnp.bfloat16
HIGHEST = lax.Precision.HIGHEST


def swap(value, axis, bits, size=4):
    return lax.ppermute(value, axis, [(i, i ^ bits) for i in range(size)])


def double(value, axis, bits):
    return jnp.concatenate([value, swap(value, axis, bits)], axis=0)


def transpose(value):
    return lax.ppermute(
        value,
        AXES,
        [
            ((((a * 4 + b) * 4 + d) * 8 + e), (((d * 4 + b) * 4 + a) * 8 + e))
            for a in range(4)
            for b in range(4)
            for d in range(4)
            for e in range(8)
        ],
    )


def spread(load, axis):
    parts = jnp.broadcast_to(load[None], (4, *load.shape))
    parts = lax.all_to_all(parts, axis, 0, 0, tiled=True)
    band = parts[0, :64] + parts[1, :64] + parts[2, :64] + parts[3, :64]
    return jnp.concatenate([band] + [parts[i, 64:] for i in range(4)], axis=0), band


def call(kernel, outs, *args, n_scalars=0, scratch=(), final=False):
    vmem = pl.BlockSpec(memory_space=pltpu.VMEM)
    smem = pl.BlockSpec(memory_space=pltpu.SMEM)
    many = isinstance(outs, tuple)
    args = args[:n_scalars] + tuple(
        pltpu.with_memory_space_constraint(a, pltpu.VMEM) for a in args[n_scalars:]
    )
    if not final:
        kept = [pltpu.VMEM(o.shape, o.dtype) for o in (outs if many else (outs,))]
        outs = tuple(kept) if many else kept[0]
    return pl.pallas_call(
        kernel,
        out_shape=outs,
        in_specs=[smem] * n_scalars + [vmem] * (len(args) - n_scalars),
        out_specs=tuple(vmem for _ in outs) if many else vmem,
        scratch_shapes=list(scratch),
    )(*args)


def dot_tn(a, b):
    return lax.dot_general(a, b, (((0,), (0,)), ((), ())), preferred_element_type=F32)


def project_kernel(mine, other, gain, p0, p1, p2, p3, keep, s1, s2, s3, column, acc, sq):
    zh, y, x, zl, c = [lax.axis_index(a) for a in AXES]
    for i, z_rel in enumerate((0, 1, 3, 2)):
        at = pl.multiple_of(64 + ((x ^ z_rel) * 4 + zl) * 64, 64)
        column[64 * i : 64 * i + 64, :] = mine[pl.ds(at, 64), :]
    total = jnp.zeros((256, 256), F32)
    squares = jnp.zeros((256, 256), F32)
    for y_rel, proj in enumerate((p0, p1, p2, p3)):
        zl_there = y ^ y_rel
        for c_rel, src in enumerate((mine, other)):
            c_there = c ^ c_rel
            rows = [
                src[pl.ds(pl.multiple_of(64 + (at_x * 4 + zl_there) * 64, 64), 64), :]
                for at_x in range(4)
            ]
            raw = jnp.concatenate(rows, axis=0).astype(F32)
            squares = squares + raw * raw
            scale = gain[pl.ds(8 * zh + 2 * zl_there + c_there, 1), :]
            scaled = (raw * scale).astype(BF16)
            weights = proj[pl.ds(pl.multiple_of(c_there * 256, 256), 256), :]
            total = total + jnp.dot(scaled, weights, preferred_element_type=F32)
    acc[...] = total
    sq[...] = jnp.broadcast_to(jnp.sum(squares, axis=1, keepdims=True), (256, 256))
    row = lax.broadcasted_iota(jnp.int32, (64, 256), 0)
    lane = lax.broadcasted_iota(jnp.int32, (64, 256), 1)
    for step, out in enumerate((keep, s1, s2, s3)):
        at = pl.multiple_of((zh ^ step) * 64, 64)
        part = acc[pl.ds(at, 64), :]
        norm = sq[pl.ds(at, 64), :]
        high = norm.astype(BF16).astype(F32)
        spread = jnp.where(lane == row, high, jnp.where(lane == row + 64, norm - high, 0.0))
        line = jnp.sum(spread, axis=0, keepdims=True)
        out[0:64, :] = part.astype(out.dtype)
        out[64:80, :] = jnp.broadcast_to(line, (16, 256)).astype(out.dtype)
        if step:
            out[80:144, :] = mine[0:64, :] + other[0:64, :]


def change_kernel(tokens, keep, r1, r2, r3, change):
    total = keep[...]
    for part in (r1, r2, r3):
        total = total + part[0:80, :].astype(F32)
    row = lax.broadcasted_iota(jnp.int32, (64, 256), 0)
    lane = lax.broadcasted_iota(jnp.int32, (64, 256), 1)
    line = jnp.broadcast_to(total[64:65, :], (64, 256))
    picked = jnp.where((lane == row) | (lane == row + 64), line, 0.0)
    square_sum = jnp.sum(picked, axis=1, keepdims=True)
    inv_rms = lax.rsqrt(square_sum / D + 1e-05)
    own = tokens[...].astype(F32)
    outputs = (own + total[0:64, :] * inv_rms).astype(BF16)
    change[...] = (outputs.astype(F32) - own).astype(BF16)


def invert_block(block):
    row = lax.broadcasted_iota(jnp.int32, (NB, 2 * NB), 0)
    lane = lax.broadcasted_iota(jnp.int32, (NB, 2 * NB), 1)
    eye = jnp.where(lane[:, :NB] == row[:, :NB], 1.0, 0.0).astype(F32)
    work = jnp.concatenate([block, eye], axis=1)
    for j in range(0, NB, STEP):
        columns = [jnp.broadcast_to(work[:, k : k + 1], work.shape) for k in range(j, j + STEP)]
        pivots = [work[k : k + 1, :] for k in range(j, j + STEP)]
        for i in range(STEP):
            scale = lax.rsqrt(columns[i][j + i : j + i + 1, :])
            pivots[i] = pivots[i] * scale
            columns[i] = columns[i] * scale
            for k in range(i + 1, STEP):
                factor = columns[i][j + k : j + k + 1, :]
                pivots[k] = pivots[k] - factor * pivots[i]
                columns[k] = columns[k] - factor * columns[i]
        update = columns[0] * pivots[0]
        for i in range(1, STEP):
            update = update + columns[i] * pivots[i]
        after = jnp.where(row >= j + STEP, work - update, work)
        for i in range(STEP):
            after = jnp.where(row == j + i, pivots[i], after)
        work = after
    return work[:, NB:]


def dot_hi(a, b, dims=((1,), (0,))):
    return lax.dot_general(a, b, (dims, ((), ())), precision=HIGHEST, preferred_element_type=F32)


def factor_kernel(b0, b1, inverse, schur):
    total = dot_tn(b0[...], b0[...]) + dot_tn(b1[...], b1[...])
    row = lax.broadcasted_iota(jnp.int32, (PANEL, PANEL), 0)
    lane = lax.broadcasted_iota(jnp.int32, (PANEL, PANEL), 1)
    schur[...] = total / TOKENS + jnp.where(row == lane, 0.1, 0.0)
    inverse[...] = jnp.where(row == lane, 1.0, 0.0)
    for k in range(PANEL // NB):
        lo, hi = k * NB, (k + 1) * NB
        block_inverse = invert_block(schur[lo:hi, lo:hi])
        top = dot_hi(block_inverse, inverse[lo:hi, :])
        inverse[lo:hi, :] = top
        if hi < PANEL:
            below = dot_hi(schur[hi:, lo:hi], block_inverse, ((1,), (1,)))
            schur[hi:, hi:] = schur[hi:, hi:] - dot_hi(below, below, ((1,), (1,)))
            inverse[hi:, :] = inverse[hi:, :] - dot_hi(below, top)


def gram_kernel(is_band, b0, b1, t0, t1, inverse, out):
    total = dot_tn(b0[...], t0[...]) + dot_tn(b1[...], t1[...])
    row = lax.broadcasted_iota(jnp.int32, (PANEL, PANEL), 0)
    lane = lax.broadcasted_iota(jnp.int32, (PANEL, PANEL), 1)
    ridge = jnp.where((row == lane) & (is_band[0] == 1), 0.1, 0.0)
    out[...] = dot_hi(inverse[...], total / TOKENS + ridge)


def cross_kernel(b0, b1, c0, c1, c2, c3, inverse, out):
    total = dot_tn(b0[0:256, :], c0[...]) + dot_tn(b0[256:512, :], c1[...])
    total = total + dot_tn(b1[0:256, :], c2[...]) + dot_tn(b1[256:512, :], c3[...])
    out[...] = dot_hi(inverse[...], total * (math.sqrt(D) / TOKENS))


def steps(tokens, gain, proj, panel_index):
    _, _, x, zl, c = [lax.axis_index(a).astype(jnp.int32) for a in AXES]
    is_band = panel_index[0].astype(jnp.int32) == 8 * x + 2 * zl + c
    band = jnp.where(is_band, tokens, jnp.zeros_like(tokens))
    gains = gain.reshape(32, 256)

    turned = transpose(tokens)
    weights = [proj] + [swap(proj, "y", k) for k in (1, 2, 3)]

    load = jnp.concatenate([band, turned], axis=0)
    load, gains = lax.optimization_barrier((load, gains))
    load, band = spread(load, "zl")
    load, band = spread(load, "x")
    other = swap(load, "c", 1, 2)
    band = band + other[:64]

    part = jax.ShapeDtypeStruct((144, 256), BF16)
    block = jax.ShapeDtypeStruct((256, 256), BF16)
    keep, s1, s2, s3, column = call(
        project_kernel,
        (jax.ShapeDtypeStruct((80, 256), F32), part, part, part, block),
        load,
        other,
        gains,
        *weights,
        scratch=(pltpu.VMEM((256, 256), F32), pltpu.VMEM((256, 256), F32)),
    )
    r2, r1, r3 = swap(s2, "zh", 2), swap(s1, "zh", 1), swap(s3, "zh", 3)
    blocks = double(transpose(column), "y", 1)
    blocks = [blocks, swap(blocks, "y", 3)]
    bands = jnp.concatenate([band] + [r[80:144] for r in (r1, r3, r2)], axis=0)
    bands = double(bands, "y", 1)
    bands = [bands, swap(bands, "y", 3)]

    change = call(change_kernel, jax.ShapeDtypeStruct((64, 256), BF16), tokens, keep, r1, r2, r3)
    change = double(change, "zh", 1)
    change = double(change, "zh", 3)
    changes = [change] + [swap(change, "y", k) for k in (1, 3, 2)]

    square = jax.ShapeDtypeStruct((PANEL, PANEL), F32)
    inverse = call(factor_kernel, square, *bands, scratch=(pltpu.VMEM((PANEL, PANEL), F32),))
    flag = is_band.astype(jnp.int32).reshape(1)
    panel_rows = call(gram_kernel, square, flag, *bands, *blocks, inverse, n_scalars=1, final=True)
    solved_cross = call(cross_kernel, square, *bands, *changes, inverse, final=True)
    return (panel_rows, solved_cross)


def solution(mesh):
    split = Mesh(np.asarray(mesh.devices).reshape(4, 4, 4, 4, 2), AXES)
    return jax.shard_map(
        steps,
        mesh=split,
        in_specs=(P(TOK, FEAT), P(), P(TOK, FEAT), P()),
        out_specs=(P(None, FEAT), P(None, FEAT)),
        check_vma=False,
    )
```

```python
import math

import jax
import jax.numpy as jnp
import numpy as np
from jax import lax
from jax.experimental import pallas as pl
from jax.experimental.pallas import tpu as pltpu
from jax.sharding import Mesh
from jax.sharding import PartitionSpec as P

D = 8192
PANEL = 256
TOKENS = 1024
AXES = ("zh", "y", "x", "zl", "c")
TOK = ("zh", "y")
FEAT = ("x", "zl", "c")
NB = 64
STEP = 16
F32 = jnp.float32
BF16 = jnp.bfloat16
HIGHEST = lax.Precision.HIGHEST


def swap(value, axis, bits, size=4):
    return lax.ppermute(value, axis, [(i, i ^ bits) for i in range(size)])


def double(value, axis, bits):
    return jnp.concatenate([value, swap(value, axis, bits)], axis=0)


def transpose(value):
    return lax.ppermute(
        value,
        AXES,
        [
            ((((a * 4 + b) * 4 + d) * 8 + e), (((d * 4 + b) * 4 + a) * 8 + e))
            for a in range(4)
            for b in range(4)
            for d in range(4)
            for e in range(8)
        ],
    )


def spread(load, axis):
    parts = jnp.broadcast_to(load[None], (4, *load.shape))
    parts = lax.all_to_all(parts, axis, 0, 0, tiled=True)
    band = parts[0, :64] + parts[1, :64] + parts[2, :64] + parts[3, :64]
    return jnp.concatenate([band] + [parts[i, 64:] for i in range(4)], axis=0), band


def call(kernel, outs, *args, n_scalars=0, scratch=(), final=False):
    vmem = pl.BlockSpec(memory_space=pltpu.VMEM)
    smem = pl.BlockSpec(memory_space=pltpu.SMEM)
    many = isinstance(outs, tuple)
    args = args[:n_scalars] + tuple(
        pltpu.with_memory_space_constraint(a, pltpu.VMEM) for a in args[n_scalars:]
    )
    if not final:
        kept = [pltpu.VMEM(o.shape, o.dtype) for o in (outs if many else (outs,))]
        outs = tuple(kept) if many else kept[0]
    return pl.pallas_call(
        kernel,
        out_shape=outs,
        in_specs=[smem] * n_scalars + [vmem] * (len(args) - n_scalars),
        out_specs=tuple(vmem for _ in outs) if many else vmem,
        scratch_shapes=list(scratch),
    )(*args)


def dot_tn(a, b):
    return lax.dot_general(a, b, (((0,), (0,)), ((), ())), preferred_element_type=F32)


def project_kernel(mine, other, gain, p0, p1, p2, p3, keep, s1, s2, s3, column, acc, sq):
    zh, y, x, zl, c = [lax.axis_index(a) for a in AXES]
    for i, z_rel in enumerate((0, 1, 3, 2)):
        at = pl.multiple_of(64 + ((x ^ z_rel) * 4 + zl) * 64, 64)
        column[64 * i : 64 * i + 64, :] = mine[pl.ds(at, 64), :]
    total = jnp.zeros((256, 256), F32)
    squares = jnp.zeros((256, 256), F32)
    for y_rel, proj in enumerate((p0, p1, p2, p3)):
        zl_there = y ^ y_rel
        for c_rel, src in enumerate((mine, other)):
            c_there = c ^ c_rel
            rows = [
                src[pl.ds(pl.multiple_of(64 + (at_x * 4 + zl_there) * 64, 64), 64), :]
                for at_x in range(4)
            ]
            raw = jnp.concatenate(rows, axis=0).astype(F32)
            squares = squares + raw * raw
            scale = gain[pl.ds(8 * zh + 2 * zl_there + c_there, 1), :]
            scaled = (raw * scale).astype(BF16)
            weights = proj[pl.ds(pl.multiple_of(c_there * 256, 256), 256), :]
            total = total + jnp.dot(scaled, weights, preferred_element_type=F32)
    acc[...] = total
    sq[...] = jnp.broadcast_to(jnp.sum(squares, axis=1, keepdims=True), (256, 256))
    row = lax.broadcasted_iota(jnp.int32, (64, 256), 0)
    lane = lax.broadcasted_iota(jnp.int32, (64, 256), 1)
    for step, out in enumerate((keep, s1, s2, s3)):
        at = pl.multiple_of((zh ^ step) * 64, 64)
        part = acc[pl.ds(at, 64), :]
        norm = sq[pl.ds(at, 64), :]
        high = norm.astype(BF16).astype(F32)
        spread = jnp.where(lane == row, high, jnp.where(lane == row + 64, norm - high, 0.0))
        line = jnp.sum(spread, axis=0, keepdims=True)
        out[0:64, :] = part.astype(out.dtype)
        out[64:80, :] = jnp.broadcast_to(line, (16, 256)).astype(out.dtype)
        if step:
            out[80:144, :] = mine[0:64, :] + other[0:64, :]


def change_kernel(tokens, keep, r1, r2, r3, change):
    total = keep[...]
    for part in (r1, r2, r3):
        total = total + part[0:80, :].astype(F32)
    row = lax.broadcasted_iota(jnp.int32, (64, 256), 0)
    lane = lax.broadcasted_iota(jnp.int32, (64, 256), 1)
    line = jnp.broadcast_to(total[64:65, :], (64, 256))
    picked = jnp.where((lane == row) | (lane == row + 64), line, 0.0)
    square_sum = jnp.sum(picked, axis=1, keepdims=True)
    inv_rms = lax.rsqrt(square_sum / D + 1e-05)
    own = tokens[...].astype(F32)
    outputs = (own + total[0:64, :] * inv_rms).astype(BF16)
    change[...] = (outputs.astype(F32) - own).astype(BF16)


def invert_block(block):
    row = lax.broadcasted_iota(jnp.int32, (NB, 2 * NB), 0)
    lane = lax.broadcasted_iota(jnp.int32, (NB, 2 * NB), 1)
    eye = jnp.where(lane[:, :NB] == row[:, :NB], 1.0, 0.0).astype(F32)
    work = jnp.concatenate([block, eye], axis=1)
    for j in range(0, NB, STEP):
        columns = [jnp.broadcast_to(work[:, k : k + 1], work.shape) for k in range(j, j + STEP)]
        pivots = [work[k : k + 1, :] for k in range(j, j + STEP)]
        for i in range(STEP):
            scale = lax.rsqrt(columns[i][j + i : j + i + 1, :])
            pivots[i] = pivots[i] * scale
            columns[i] = columns[i] * scale
            for k in range(i + 1, STEP):
                factor = columns[i][j + k : j + k + 1, :]
                pivots[k] = pivots[k] - factor * pivots[i]
                columns[k] = columns[k] - factor * columns[i]
        update = columns[0] * pivots[0]
        for i in range(1, STEP):
            update = update + columns[i] * pivots[i]
        after = jnp.where(row >= j + STEP, work - update, work)
        for i in range(STEP):
            after = jnp.where(row == j + i, pivots[i], after)
        work = after
    return work[:, NB:]


def dot_hi(a, b, dims=((1,), (0,))):
    return lax.dot_general(a, b, (dims, ((), ())), precision=HIGHEST, preferred_element_type=F32)


def factor_kernel(b0, b1, inverse, schur):
    total = dot_tn(b0[...], b0[...]) + dot_tn(b1[...], b1[...])
    row = lax.broadcasted_iota(jnp.int32, (PANEL, PANEL), 0)
    lane = lax.broadcasted_iota(jnp.int32, (PANEL, PANEL), 1)
    schur[...] = total / TOKENS + jnp.where(row == lane, 0.1, 0.0)
    inverse[...] = jnp.where(row == lane, 1.0, 0.0)
    for k in range(PANEL // NB):
        lo, hi = k * NB, (k + 1) * NB
        block_inverse = invert_block(schur[lo:hi, lo:hi])
        top = dot_hi(block_inverse, inverse[lo:hi, :])
        inverse[lo:hi, :] = top
        if hi < PANEL:
            below = dot_hi(schur[hi:, lo:hi], block_inverse, ((1,), (1,)))
            schur[hi:, hi:] = schur[hi:, hi:] - dot_hi(below, below, ((1,), (1,)))
            inverse[hi:, :] = inverse[hi:, :] - dot_hi(below, top)


def solve_kernel(is_band, near, far, both, inverse, panel_rows, solved_cross):
    y = lax.axis_index("y")
    total = dot_tn(near[0:256, :], both[y])
    total = total + dot_tn(near[256:512, :], both[y ^ 1])
    total = total + dot_tn(far[0:256, :], both[y ^ 3])
    total = total + dot_tn(far[256:512, :], both[y ^ 2])
    row = lax.broadcasted_iota(jnp.int32, (PANEL, PANEL), 0)
    lane = lax.broadcasted_iota(jnp.int32, (PANEL, PANEL), 1)
    ridge = jnp.where((row == lane) & (is_band[0] == 1), 0.1, 0.0)
    panel_rows[...] = dot_hi(inverse[...], total[:, 256:512] / TOKENS + ridge)
    solved_cross[...] = dot_hi(inverse[...], total[:, 0:256] * (math.sqrt(D) / TOKENS))


def steps(tokens, gain, proj, panel_index):
    _, _, x, zl, c = [lax.axis_index(a).astype(jnp.int32) for a in AXES]
    is_band = panel_index[0].astype(jnp.int32) == 8 * x + 2 * zl + c
    band = jnp.where(is_band, tokens, jnp.zeros_like(tokens))
    gains = gain.reshape(32, 256)

    turned = transpose(tokens)
    weights = [proj] + [swap(proj, "y", k) for k in (1, 2, 3)]

    load = jnp.concatenate([band, turned], axis=0)
    load, gains = lax.optimization_barrier((load, gains))
    load, band = spread(load, "zl")
    load, band = spread(load, "x")
    other = swap(load, "c", 1, 2)
    band = band + other[:64]

    part = jax.ShapeDtypeStruct((144, 256), BF16)
    block = jax.ShapeDtypeStruct((256, 256), BF16)
    keep, s1, s2, s3, column = call(
        project_kernel,
        (jax.ShapeDtypeStruct((80, 256), F32), part, part, part, block),
        load,
        other,
        gains,
        *weights,
        scratch=(pltpu.VMEM((256, 256), F32), pltpu.VMEM((256, 256), F32)),
    )
    r2, r1, r3 = swap(s2, "zh", 2), swap(s1, "zh", 1), swap(s3, "zh", 3)
    column = transpose(column)
    bands = jnp.concatenate([band] + [r[80:144] for r in (r1, r3, r2)], axis=0)
    bands = double(bands, "y", 1)
    bands = [bands, swap(bands, "y", 3)]

    change = call(change_kernel, jax.ShapeDtypeStruct((64, 256), BF16), tokens, keep, r1, r2, r3)
    change = double(change, "zh", 1)
    change = double(change, "zh", 3)
    both = jnp.concatenate([change, column], axis=1)
    both = jnp.broadcast_to(both[None], (4, *both.shape))
    both = lax.all_to_all(both, "y", 0, 0, tiled=True)

    square = jax.ShapeDtypeStruct((PANEL, PANEL), F32)
    inverse = call(factor_kernel, square, *bands, scratch=(pltpu.VMEM((PANEL, PANEL), F32),))
    flag = is_band.astype(jnp.int32).reshape(1)
    panel_rows, solved_cross = call(
        solve_kernel, (square, square), flag, *bands, both, inverse, n_scalars=1, final=True
    )
    return (panel_rows, solved_cross)


def solution(mesh):
    split = Mesh(np.asarray(mesh.devices).reshape(4, 4, 4, 4, 2), AXES)
    return jax.shard_map(
        steps,
        mesh=split,
        in_specs=(P(TOK, FEAT), P(), P(TOK, FEAT), P()),
        out_specs=(P(None, FEAT), P(None, FEAT)),
        check_vma=False,
    )
```

```python
import math

import jax
import jax.numpy as jnp
import numpy as np
from jax import lax
from jax.experimental import pallas as pl
from jax.experimental.pallas import tpu as pltpu
from jax.sharding import Mesh
from jax.sharding import PartitionSpec as P

D = 8192
PANEL = 256
TOKENS = 1024
AXES = ("zh", "y", "x", "zl", "c")
TOK = ("zh", "y")
FEAT = ("x", "zl", "c")
NB = 64
STEP = 16
F32 = jnp.float32
BF16 = jnp.bfloat16
HIGHEST = lax.Precision.HIGHEST


def swap(value, axis, bits, size=4):
    return lax.ppermute(value, axis, [(i, i ^ bits) for i in range(size)])


def double(value, axis, bits):
    return jnp.concatenate([value, swap(value, axis, bits)], axis=0)


def transpose(value):
    return lax.ppermute(
        value,
        AXES,
        [
            ((((a * 4 + b) * 4 + d) * 8 + e), (((d * 4 + b) * 4 + a) * 8 + e))
            for a in range(4)
            for b in range(4)
            for d in range(4)
            for e in range(8)
        ],
    )


def spread(load, axis):
    parts = jnp.broadcast_to(load[None], (4, *load.shape))
    parts = lax.all_to_all(parts, axis, 0, 0, tiled=True)
    band = parts[0, :64] + parts[1, :64] + parts[2, :64] + parts[3, :64]
    return jnp.concatenate([band] + [parts[i, 64:] for i in range(4)], axis=0), band


def call(kernel, outs, *args, n_scalars=0, scratch=(), final=False):
    vmem = pl.BlockSpec(memory_space=pltpu.VMEM)
    smem = pl.BlockSpec(memory_space=pltpu.SMEM)
    many = isinstance(outs, tuple)
    args = args[:n_scalars] + tuple(
        pltpu.with_memory_space_constraint(a, pltpu.VMEM) for a in args[n_scalars:]
    )
    if not final:
        kept = [pltpu.VMEM(o.shape, o.dtype) for o in (outs if many else (outs,))]
        outs = tuple(kept) if many else kept[0]
    return pl.pallas_call(
        kernel,
        out_shape=outs,
        in_specs=[smem] * n_scalars + [vmem] * (len(args) - n_scalars),
        out_specs=tuple(vmem for _ in outs) if many else vmem,
        scratch_shapes=list(scratch),
    )(*args)


def dot_tn(a, b):
    return lax.dot_general(a, b, (((0,), (0,)), ((), ())), preferred_element_type=F32)


def project_kernel(mine, other, gain, own, p0, p1, p2, p3, keep, s1, s2, s3, acc, sq):
    zh, y, c = [lax.axis_index(a) for a in ("zh", "y", "c")]
    total = jnp.zeros((256, 256), F32)
    squares = jnp.zeros((256, 256), F32)
    for y_rel, proj in enumerate((p0, p1, p2, p3)):
        zl_there = y ^ y_rel
        for c_rel, src in enumerate((mine, other)):
            c_there = c ^ c_rel
            rows = [
                src[pl.ds(pl.multiple_of(64 + (at_x * 4 + zl_there) * 64, 64), 64), :]
                for at_x in range(4)
            ]
            raw = jnp.concatenate(rows, axis=0).astype(F32)
            squares = squares + raw * raw
            scale = gain[pl.ds(8 * zh + 2 * zl_there + c_there, 1), :]
            scaled = (raw * scale).astype(BF16)
            weights = proj[pl.ds(pl.multiple_of(c_there * 256, 256), 256), :]
            total = total + jnp.dot(scaled, weights, preferred_element_type=F32)
    acc[...] = total
    sq[...] = jnp.broadcast_to(jnp.sum(squares, axis=1, keepdims=True), (256, 256))
    row = lax.broadcasted_iota(jnp.int32, (64, 256), 0)
    lane = lax.broadcasted_iota(jnp.int32, (64, 256), 1)
    for step, out in enumerate((keep, s1, s2, s3)):
        at = pl.multiple_of((zh ^ step) * 64, 64)
        part = acc[pl.ds(at, 64), :]
        norm = sq[pl.ds(at, 64), :]
        high = norm.astype(BF16).astype(F32)
        spread = jnp.where(lane == row, high, jnp.where(lane == row + 64, norm - high, 0.0))
        line = jnp.sum(spread, axis=0, keepdims=True)
        out[0:64, :] = part.astype(out.dtype)
        out[64:80, :] = jnp.broadcast_to(line, (16, 256)).astype(out.dtype)
        if step:
            out[80:144, :] = mine[0:64, :] + other[0:64, :]
            out[144:208, :] = own[...]


def change_kernel(tokens, keep, r1, r2, r3, change):
    total = keep[...]
    for part in (r1, r2, r3):
        total = total + part[0:80, :].astype(F32)
    row = lax.broadcasted_iota(jnp.int32, (64, 256), 0)
    lane = lax.broadcasted_iota(jnp.int32, (64, 256), 1)
    line = jnp.broadcast_to(total[64:65, :], (64, 256))
    picked = jnp.where((lane == row) | (lane == row + 64), line, 0.0)
    square_sum = jnp.sum(picked, axis=1, keepdims=True)
    inv_rms = lax.rsqrt(square_sum / D + 1e-05)
    own = tokens[...].astype(F32)
    outputs = (own + total[0:64, :] * inv_rms).astype(BF16)
    change[...] = (outputs.astype(F32) - own).astype(BF16)


def invert_block(block):
    row = lax.broadcasted_iota(jnp.int32, (NB, 2 * NB), 0)
    lane = lax.broadcasted_iota(jnp.int32, (NB, 2 * NB), 1)
    eye = jnp.where(lane[:, :NB] == row[:, :NB], 1.0, 0.0).astype(F32)
    work = jnp.concatenate([block, eye], axis=1)
    for j in range(0, NB, STEP):
        columns = [jnp.broadcast_to(work[:, k : k + 1], work.shape) for k in range(j, j + STEP)]
        pivots = [work[k : k + 1, :] for k in range(j, j + STEP)]
        for i in range(STEP):
            scale = lax.rsqrt(columns[i][j + i : j + i + 1, :])
            pivots[i] = pivots[i] * scale
            columns[i] = columns[i] * scale
            for k in range(i + 1, STEP):
                factor = columns[i][j + k : j + k + 1, :]
                pivots[k] = pivots[k] - factor * pivots[i]
                columns[k] = columns[k] - factor * columns[i]
        update = columns[0] * pivots[0]
        for i in range(1, STEP):
            update = update + columns[i] * pivots[i]
        after = jnp.where(row >= j + STEP, work - update, work)
        for i in range(STEP):
            after = jnp.where(row == j + i, pivots[i], after)
        work = after
    return work[:, NB:]


def dot_hi(a, b, dims=((1,), (0,))):
    return lax.dot_general(a, b, (dims, ((), ())), precision=HIGHEST, preferred_element_type=F32)


def factor_kernel(b0, b1, inverse, schur):
    total = dot_tn(b0[...], b0[...]) + dot_tn(b1[...], b1[...])
    row = lax.broadcasted_iota(jnp.int32, (PANEL, PANEL), 0)
    lane = lax.broadcasted_iota(jnp.int32, (PANEL, PANEL), 1)
    schur[...] = total / TOKENS + jnp.where(row == lane, 0.1, 0.0)
    inverse[...] = jnp.where(row == lane, 1.0, 0.0)
    for k in range(PANEL // NB):
        lo, hi = k * NB, (k + 1) * NB
        block_inverse = invert_block(schur[lo:hi, lo:hi])
        top = dot_hi(block_inverse, inverse[lo:hi, :])
        inverse[lo:hi, :] = top
        if hi < PANEL:
            below = dot_hi(schur[hi:, lo:hi], block_inverse, ((1,), (1,)))
            schur[hi:, hi:] = schur[hi:, hi:] - dot_hi(below, below, ((1,), (1,)))
            inverse[hi:, :] = inverse[hi:, :] - dot_hi(below, top)


def solve_kernel(is_band, near, far, both, inverse, panel_rows, solved_cross):
    y = lax.axis_index("y")
    total = dot_tn(near[0:256, :], both[y])
    total = total + dot_tn(near[256:512, :], both[y ^ 1])
    total = total + dot_tn(far[0:256, :], both[y ^ 3])
    total = total + dot_tn(far[256:512, :], both[y ^ 2])
    row = lax.broadcasted_iota(jnp.int32, (PANEL, PANEL), 0)
    lane = lax.broadcasted_iota(jnp.int32, (PANEL, PANEL), 1)
    ridge = jnp.where((row == lane) & (is_band[0] == 1), 0.1, 0.0)
    panel_rows[...] = dot_hi(inverse[...], total[:, 256:512] / TOKENS + ridge)
    solved_cross[...] = dot_hi(inverse[...], total[:, 0:256] * (math.sqrt(D) / TOKENS))


def steps(tokens, gain, proj, panel_index):
    _, _, x, zl, c = [lax.axis_index(a).astype(jnp.int32) for a in AXES]
    is_band = panel_index[0].astype(jnp.int32) == 8 * x + 2 * zl + c
    band = jnp.where(is_band, tokens, jnp.zeros_like(tokens))
    gains = gain.reshape(32, 256)

    turned = transpose(tokens)
    weights = [proj] + [swap(proj, "y", k) for k in (1, 2, 3)]

    load = jnp.concatenate([band, turned], axis=0)
    load, gains = lax.optimization_barrier((load, gains))
    load, band = spread(load, "zl")
    load, band = spread(load, "x")
    other = swap(load, "c", 1, 2)
    band = band + other[:64]

    part = jax.ShapeDtypeStruct((208, 256), BF16)
    keep, s1, s2, s3 = call(
        project_kernel,
        (jax.ShapeDtypeStruct((80, 256), F32), part, part, part),
        load,
        other,
        gains,
        tokens,
        *weights,
        scratch=(pltpu.VMEM((256, 256), F32), pltpu.VMEM((256, 256), F32)),
    )
    r2, r1, r3 = swap(s2, "zh", 2), swap(s1, "zh", 1), swap(s3, "zh", 3)
    column = jnp.concatenate([tokens] + [r[144:208] for r in (r1, r3, r2)], axis=0)
    bands = jnp.concatenate([band] + [r[80:144] for r in (r1, r3, r2)], axis=0)
    bands = double(bands, "y", 1)
    bands = [bands, swap(bands, "y", 3)]

    change = call(change_kernel, jax.ShapeDtypeStruct((64, 256), BF16), tokens, keep, r1, r2, r3)
    change = double(change, "zh", 1)
    change = double(change, "zh", 3)
    both = jnp.concatenate([change, column], axis=1)
    both = jnp.broadcast_to(both[None], (4, *both.shape))
    both = lax.all_to_all(both, "y", 0, 0, tiled=True)

    square = jax.ShapeDtypeStruct((PANEL, PANEL), F32)
    inverse = call(factor_kernel, square, *bands, scratch=(pltpu.VMEM((PANEL, PANEL), F32),))
    flag = is_band.astype(jnp.int32).reshape(1)
    panel_rows, solved_cross = call(
        solve_kernel, (square, square), flag, *bands, both, inverse, n_scalars=1, final=True
    )
    return (panel_rows, solved_cross)


def solution(mesh):
    split = Mesh(np.asarray(mesh.devices).reshape(4, 4, 4, 4, 2), AXES)
    return jax.shard_map(
        steps,
        mesh=split,
        in_specs=(P(TOK, FEAT), P(), P(TOK, FEAT), P()),
        out_specs=(P(None, FEAT), P(None, FEAT)),
        check_vma=False,
    )
```

```python
import math

import jax
import jax.numpy as jnp
import numpy as np
from jax import lax
from jax.experimental import pallas as pl
from jax.experimental.pallas import tpu as pltpu
from jax.sharding import Mesh
from jax.sharding import PartitionSpec as P

D = 8192
PANEL = 256
TOKENS = 1024
AXES = ("zh", "y", "x", "zl", "c")
TOK = ("zh", "y")
FEAT = ("x", "zl", "c")
NB = 64
STEP = 16
F32 = jnp.float32
BF16 = jnp.bfloat16
HIGHEST = lax.Precision.HIGHEST


def swap(value, axis, bits, size=4):
    return lax.ppermute(value, axis, [(i, i ^ bits) for i in range(size)])


def double(value, axis, bits):
    return jnp.concatenate([value, swap(value, axis, bits)], axis=0)


def transpose(value):
    return lax.ppermute(
        value,
        AXES,
        [
            ((((a * 4 + b) * 4 + d) * 8 + e), (((d * 4 + b) * 4 + a) * 8 + e))
            for a in range(4)
            for b in range(4)
            for d in range(4)
            for e in range(8)
        ],
    )


def spread(load, axis):
    parts = jnp.broadcast_to(load[None], (4, *load.shape))
    parts = lax.all_to_all(parts, axis, 0, 0, tiled=True)
    band = parts[0, :64] + parts[1, :64] + parts[2, :64] + parts[3, :64]
    return jnp.concatenate([band] + [parts[i, 64:] for i in range(4)], axis=0), band


def call(kernel, outs, *args, n_scalars=0, scratch=(), final=False):
    vmem = pl.BlockSpec(memory_space=pltpu.VMEM)
    smem = pl.BlockSpec(memory_space=pltpu.SMEM)
    many = isinstance(outs, tuple)
    args = args[:n_scalars] + tuple(
        pltpu.with_memory_space_constraint(a, pltpu.VMEM) for a in args[n_scalars:]
    )
    if not final:
        kept = [pltpu.VMEM(o.shape, o.dtype) for o in (outs if many else (outs,))]
        outs = tuple(kept) if many else kept[0]
    return pl.pallas_call(
        kernel,
        out_shape=outs,
        in_specs=[smem] * n_scalars + [vmem] * (len(args) - n_scalars),
        out_specs=tuple(vmem for _ in outs) if many else vmem,
        scratch_shapes=list(scratch),
    )(*args)


def dot_tn(a, b):
    return lax.dot_general(a, b, (((0,), (0,)), ((), ())), preferred_element_type=F32)


def project_kernel(mine, other, gain, own, p0, p1, p2, p3, keep, s1, s2, s3, acc, sq):
    zh, y, c = [lax.axis_index(a) for a in ("zh", "y", "c")]
    total = jnp.zeros((256, 256), F32)
    squares = jnp.zeros((256, 256), F32)
    for y_rel, proj in enumerate((p0, p1, p2, p3)):
        zl_there = y ^ y_rel
        for c_rel, src in enumerate((mine, other)):
            c_there = c ^ c_rel
            rows = [
                src[pl.ds(pl.multiple_of(64 + (at_x * 4 + zl_there) * 64, 64), 64), :]
                for at_x in range(4)
            ]
            raw = jnp.concatenate(rows, axis=0).astype(F32)
            squares = squares + raw * raw
            scale = gain[pl.ds(8 * zh + 2 * zl_there + c_there, 1), :]
            scaled = (raw * scale).astype(BF16)
            weights = proj[pl.ds(pl.multiple_of(c_there * 256, 256), 256), :]
            total = total + jnp.dot(scaled, weights, preferred_element_type=F32)
    acc[...] = total
    sq[...] = jnp.broadcast_to(jnp.sum(squares, axis=1, keepdims=True), (256, 256))
    row = lax.broadcasted_iota(jnp.int32, (64, 256), 0)
    lane = lax.broadcasted_iota(jnp.int32, (64, 256), 1)
    for step, out in enumerate((keep, s1, s2, s3)):
        at = pl.multiple_of((zh ^ step) * 64, 64)
        part = acc[pl.ds(at, 64), :]
        norm = sq[pl.ds(at, 64), :]
        high = norm.astype(BF16).astype(F32)
        spread = jnp.where(lane == row, high, jnp.where(lane == row + 64, norm - high, 0.0))
        line = jnp.sum(spread, axis=0, keepdims=True)
        out[0:64, :] = part.astype(out.dtype)
        out[64:80, :] = jnp.broadcast_to(line, (16, 256)).astype(out.dtype)
        if step:
            out[80:144, :] = mine[0:64, :] + other[0:64, :]
        if step in (1, 3):
            out[144:208, :] = own[...]


def change_kernel(tokens, keep, r1, r2, r3, change):
    total = keep[...]
    for part in (r1, r2, r3):
        total = total + part[0:80, :].astype(F32)
    row = lax.broadcasted_iota(jnp.int32, (64, 256), 0)
    lane = lax.broadcasted_iota(jnp.int32, (64, 256), 1)
    line = jnp.broadcast_to(total[64:65, :], (64, 256))
    picked = jnp.where((lane == row) | (lane == row + 64), line, 0.0)
    square_sum = jnp.sum(picked, axis=1, keepdims=True)
    inv_rms = lax.rsqrt(square_sum / D + 1e-05)
    own = tokens[...].astype(F32)
    outputs = (own + total[0:64, :] * inv_rms).astype(BF16)
    change[...] = (outputs.astype(F32) - own).astype(BF16)


def invert_block(block):
    row = lax.broadcasted_iota(jnp.int32, (NB, 2 * NB), 0)
    lane = lax.broadcasted_iota(jnp.int32, (NB, 2 * NB), 1)
    eye = jnp.where(lane[:, :NB] == row[:, :NB], 1.0, 0.0).astype(F32)
    work = jnp.concatenate([block, eye], axis=1)
    for j in range(0, NB, STEP):
        columns = [jnp.broadcast_to(work[:, k : k + 1], work.shape) for k in range(j, j + STEP)]
        pivots = [work[k : k + 1, :] for k in range(j, j + STEP)]
        for i in range(STEP):
            scale = lax.rsqrt(columns[i][j + i : j + i + 1, :])
            pivots[i] = pivots[i] * scale
            columns[i] = columns[i] * scale
            for k in range(i + 1, STEP):
                factor = columns[i][j + k : j + k + 1, :]
                pivots[k] = pivots[k] - factor * pivots[i]
                columns[k] = columns[k] - factor * columns[i]
        update = columns[0] * pivots[0]
        for i in range(1, STEP):
            update = update + columns[i] * pivots[i]
        after = jnp.where(row >= j + STEP, work - update, work)
        for i in range(STEP):
            after = jnp.where(row == j + i, pivots[i], after)
        work = after
    return work[:, NB:]


def dot_hi(a, b, dims=((1,), (0,))):
    return lax.dot_general(a, b, (dims, ((), ())), precision=HIGHEST, preferred_element_type=F32)


def factor_kernel(b0, b1, inverse, schur):
    total = dot_tn(b0[...], b0[...]) + dot_tn(b1[...], b1[...])
    row = lax.broadcasted_iota(jnp.int32, (PANEL, PANEL), 0)
    lane = lax.broadcasted_iota(jnp.int32, (PANEL, PANEL), 1)
    schur[...] = total / TOKENS + jnp.where(row == lane, 0.1, 0.0)
    inverse[...] = jnp.where(row == lane, 1.0, 0.0)
    for k in range(PANEL // NB):
        lo, hi = k * NB, (k + 1) * NB
        block_inverse = invert_block(schur[lo:hi, lo:hi])
        top = dot_hi(block_inverse, inverse[lo:hi, :])
        inverse[lo:hi, :] = top
        if hi < PANEL:
            below = dot_hi(schur[hi:, lo:hi], block_inverse, ((1,), (1,)))
            schur[hi:, hi:] = schur[hi:, hi:] - dot_hi(below, below, ((1,), (1,)))
            inverse[hi:, :] = inverse[hi:, :] - dot_hi(below, top)


def solve_kernel(is_band, near, far, both, inverse, panel_rows, solved_cross):
    y = lax.axis_index("y")
    total = dot_tn(near[0:256, :], both[y])
    total = total + dot_tn(near[256:512, :], both[y ^ 1])
    total = total + dot_tn(far[0:256, :], both[y ^ 3])
    total = total + dot_tn(far[256:512, :], both[y ^ 2])
    row = lax.broadcasted_iota(jnp.int32, (PANEL, PANEL), 0)
    lane = lax.broadcasted_iota(jnp.int32, (PANEL, PANEL), 1)
    ridge = jnp.where((row == lane) & (is_band[0] == 1), 0.1, 0.0)
    panel_rows[...] = dot_hi(inverse[...], total[:, 256:512] / TOKENS + ridge)
    solved_cross[...] = dot_hi(inverse[...], total[:, 0:256] * (math.sqrt(D) / TOKENS))


def steps(tokens, gain, proj, panel_index):
    _, _, x, zl, c = [lax.axis_index(a).astype(jnp.int32) for a in AXES]
    is_band = panel_index[0].astype(jnp.int32) == 8 * x + 2 * zl + c
    band = jnp.where(is_band, tokens, jnp.zeros_like(tokens))
    gains = gain.reshape(32, 256)

    turned = transpose(tokens)
    weights = [proj] + [swap(proj, "y", k) for k in (1, 2, 3)]

    load = jnp.concatenate([band, turned], axis=0)
    load, gains = lax.optimization_barrier((load, gains))
    load, band = spread(load, "zl")
    load, band = spread(load, "x")
    other = swap(load, "c", 1, 2)
    band = band + other[:64]

    part = jax.ShapeDtypeStruct((208, 256), BF16)
    short = jax.ShapeDtypeStruct((144, 256), BF16)
    keep, s1, s2, s3 = call(
        project_kernel,
        (jax.ShapeDtypeStruct((80, 256), F32), part, short, part),
        load,
        other,
        gains,
        tokens,
        *weights,
        scratch=(pltpu.VMEM((256, 256), F32), pltpu.VMEM((256, 256), F32)),
    )
    r2, r1, r3 = swap(s2, "zh", 2), swap(s1, "zh", 1), swap(s3, "zh", 3)
    bands = jnp.concatenate([band] + [r[80:144] for r in (r1, r3, r2)], axis=0)
    bands = double(bands, "y", 1)
    bands = [bands, swap(bands, "y", 3)]

    change = call(change_kernel, jax.ShapeDtypeStruct((64, 256), BF16), tokens, keep, r1, r2, r3)
    there = swap(jnp.concatenate([change, r3[144:208]], axis=0), "zh", 1)
    change = jnp.concatenate([change, there[:64]], axis=0)
    column = jnp.concatenate([tokens, r1[144:208], r3[144:208], there[64:]], axis=0)
    change = double(change, "zh", 3)
    both = jnp.concatenate([change, column], axis=1)
    both = jnp.broadcast_to(both[None], (4, *both.shape))
    both = lax.all_to_all(both, "y", 0, 0, tiled=True)

    square = jax.ShapeDtypeStruct((PANEL, PANEL), F32)
    inverse = call(factor_kernel, square, *bands, scratch=(pltpu.VMEM((PANEL, PANEL), F32),))
    flag = is_band.astype(jnp.int32).reshape(1)
    panel_rows, solved_cross = call(
        solve_kernel, (square, square), flag, *bands, both, inverse, n_scalars=1, final=True
    )
    return (panel_rows, solved_cross)


def solution(mesh):
    split = Mesh(np.asarray(mesh.devices).reshape(4, 4, 4, 4, 2), AXES)
    return jax.shard_map(
        steps,
        mesh=split,
        in_specs=(P(TOK, FEAT), P(), P(TOK, FEAT), P()),
        out_specs=(P(None, FEAT), P(None, FEAT)),
        check_vma=False,
    )
```
